32 devices in a mesh: mem: 8 (over y, x, core), st: 4 (over z).
Axes of the slice: x: 2, y: 2, z: 4, core: 2. Of those that a mesh axis runs over, the one named last changes fastest.
Arguments:
- ensemble: float32 [8192, 256], P('st', 'mem'), may hold values from -8 to 8
- obs_values: float32 [4, 8, 128], replicated, may hold values from -8 to 8
- obs_sigma: float32 [4, 8, 128], replicated, may hold values from 0.25 to 0.5
- obs_operator: float32 [4, 8, 2, 128, 128], replicated, may hold values from -0.375 to 0.375
- block_cols: int32 [4, 8, 2], replicated, may hold values from 0 to 63
- batch_order: int32 [4], replicated, may hold values from 0 to 3, each once
Outputs:
- analysis: float32 [8192, 256], P('st', 'mem')
- log_weights: float32 [256], P('mem')
- ess: float32 [], replicated
The draws below stay inside these ranges and needn't reach their ends.
Inputs may be any that keep to these rules, and one draw needn't show every extreme that they name: `block_cols`: block indices of the whole state. `batch_order`: each batch exactly once.
All inputs are finite; a program needn't handle non-finite values.
Results may differ from the reference program's by a relative error of at most 0.0003.
Values sent between devices are 32-bit elements; how exact they have to be, the bound alone decides.
A program may use at most 64 MiB of HBM per device.

```python
import math
import jax
import jax.numpy as jnp
from jax import lax

SBLK = 128
OB = 8
KB = 2
NBATCH = 4
MEMBERS = 256
NBLK = 64
STATE = 8192
NOBS = 4096


mode_count = 64


def draw_ensemble(key, part):
    base_key = jax.random.fold_in(key, 11)
    load_key = jax.random.fold_in(key, 12)
    series_key = jax.random.fold_in(key, 13)
    base = jax.random.normal(base_key, (STATE, MEMBERS), jnp.float32)
    loadings = jax.random.normal(load_key, (STATE, mode_count), jnp.float32)
    series = jax.random.normal(series_key, (mode_count, MEMBERS), jnp.float32)
    amplitude = jnp.exp2(-jnp.arange(mode_count, dtype=jnp.float32) / 6.0)

    def add_mode(index, total):
        column = lax.dynamic_index_in_dim(loadings, index, 1, keepdims=False)
        row = lax.dynamic_index_in_dim(series, index, 0, keepdims=False)
        scale = lax.dynamic_index_in_dim(amplitude, index, 0, keepdims=False)
        return total + scale * column[:, None] * row[None, :]
    total = lax.fori_loop(0, mode_count, add_mode, 0.5 * base)
    return jnp.clip(total, -8.0, 8.0).astype(jnp.float32)


def touch_ends(entries, own_key, least, high):
    longest = entries.shape.index(max(entries.shape))
    spots = []
    for shift in (0, 1):
        where = [jax.random.randint(jax.random.fold_in(own_key, axis), (), 0, length) for axis, length in enumerate(entries.shape)]
        where[longest] = (where[longest] + shift) % entries.shape[longest]
        spots.append(tuple(where))
    return entries.at[spots[0]].set(least).at[spots[1]].set(high)


def centred(stream_key, extent, spread, limit, kind=jnp.bfloat16):
    drawn = spread * jax.random.normal(stream_key, extent, jnp.float32)
    return jnp.clip(drawn, min=-limit, max=limit).astype(kind)


def setup_inputs(seed: int = 0) -> dict:
    seeds = jax.random.split(jax.random.key(seed), 7)
    ensemble = draw_ensemble(jax.random.fold_in(seeds[6], 71), 0)
    obs_values = centred(seeds[1], (NBATCH, OB, SBLK), 1.5, 8.0, jnp.float32)
    obs_sigma = jnp.clip(jnp.exp(jax.random.uniform(seeds[2], (NBATCH, OB, SBLK), jnp.float32, math.log(0.25), math.log(0.5))), 0.25, 0.5)
    obs_operator = centred(seeds[3], (NBATCH, OB, KB, SBLK, SBLK), (KB * SBLK) ** -0.5, 0.375, jnp.float32)
    block_cols = touch_ends(jax.random.randint(seeds[4], (NBATCH, OB, KB), 0, NBLK), jax.random.fold_in(seeds[4], 1), 0, NBLK - 1).astype(jnp.int32)
    batch_order = jax.random.permutation(seeds[5], NBATCH).astype(jnp.int32)
    return dict(ensemble=ensemble, obs_values=obs_values, obs_sigma=obs_sigma, obs_operator=obs_operator, block_cols=block_cols, batch_order=batch_order)


precise = lax.Precision.HIGHEST

def solve_blocks(moment, target):
    factor = jnp.linalg.cholesky(moment)
    return jax.vmap(lambda lower, right: jax.scipy.linalg.cho_solve((lower, True), right))(factor, target)

def reference(ensemble, obs_values, obs_sigma, obs_operator, block_cols, batch_order):
    states = ensemble.reshape(NBLK, SBLK, MEMBERS)
    loglik = jnp.zeros((MEMBERS,), jnp.float32)
    temper = 1.0 / math.sqrt(NOBS)
    eye = jnp.eye(SBLK, dtype=jnp.float32)
    for batch_step in range(NBATCH):
        chosen = batch_order[batch_step]
        operator_now = obs_operator[chosen]
        columns = block_cols[chosen].astype(jnp.int32)
        values_now = obs_values[chosen]
        sigma_now = obs_sigma[chosen]
        picked = states[columns]
        image = jnp.einsum('bkij,bkjm->bim', operator_now, picked, precision=precise)
        center = lax.optimization_barrier(jnp.sum(image, axis=2)) / MEMBERS
        anomaly = image - center[:, :, None]
        misfit = (values_now[:, :, None] - image) / sigma_now[:, :, None]
        loglik = loglik - 0.5 * temper * lax.optimization_barrier(jnp.sum(misfit * misfit, axis=(0, 1)))
        moment = jnp.einsum('bim,bjm->bij', anomaly, anomaly, precision=precise) / (MEMBERS - 1)
        moment = moment + eye * (sigma_now * sigma_now)[:, :, None]
        cross = jnp.einsum('bkim,bjm->bkij', picked, anomaly, precision=precise) / (MEMBERS - 1)
        target = (values_now - center)[:, :, None] - 0.5 * anomaly
        weights = solve_blocks(moment, target)
        change = jnp.einsum('bkij,bjm->bkim', cross, weights, precision=precise)
        states = states.at[columns.reshape(-1)].add(change.reshape(-1, SBLK, MEMBERS))
    largest = jnp.max(loglik)
    scaled = jnp.exp(loglik - largest)
    summed = jnp.sum(scaled)
    squares = jnp.sum(scaled * scaled)
    log_weights = loglik - largest - jnp.log(summed)
    ess = summed * summed / squares
    return (states.reshape(STATE, MEMBERS), log_weights, ess)
```

```python
import functools
import math

import jax
import jax.numpy as jnp
from jax import lax
from jax.experimental import pallas as pl
from jax.experimental.pallas import tpu as pltpu
from jax.sharding import PartitionSpec as P

precise = lax.Precision.HIGHEST
PANEL = 16
GATHER_LIMIT = 16 << 20


def dot_nt(a, b):
    return lax.dot_general(a, b, (((1,), (1,)), ((), ())), precision=precise, preferred_element_type=jnp.float32)


def dot_tn(a, b):
    return lax.dot_general(a, b, (((0,), (0,)), ((), ())), precision=precise, preferred_element_type=jnp.float32)


def dot_nn(a, b):
    return lax.dot_general(a, b, (((1,), (0,)), ((), ())), precision=precise, preferred_element_type=jnp.float32)


def sweep_panel(moments, pivots, obs_blocks, size, panel):
    first = panel * PANEL
    lanes = lax.broadcasted_iota(jnp.int32, (obs_blocks, size), 1)
    entry = {}
    for i in range(PANEL):
        start = pl.multiple_of((first + i) * obs_blocks, obs_blocks)
        row = pltpu.roll(moments[pl.ds(start, obs_blocks), :], size - first, 1)
        for j in range(i + 1):
            entry[i, j] = jnp.broadcast_to(row[:, j : j + 1], (obs_blocks, size))

    def at(i, j):
        return (i, j) if i >= j else (j, i)

    for p in range(PANEL):
        inverse = 1.0 / entry[p, p]
        column = {i: entry[at(i, p)] for i in range(PANEL) if i != p}
        scaled = {i: column[i] * inverse for i in column}
        for i in column:
            for j in column:
                if j <= i:
                    entry[i, j] = entry[i, j] - scaled[i] * column[j]
        for i in column:
            entry[at(i, p)] = scaled[i]
        entry[p, p] = -inverse
    for i in range(PANEL):
        placed = jnp.zeros((obs_blocks, size), jnp.float32)
        for j in range(PANEL):
            placed = jnp.where(lanes == first + j, entry[at(i, j)], placed)
        pivots[i * obs_blocks : (i + 1) * obs_blocks, :] = placed

    cols = lax.broadcasted_iota(jnp.int32, (size, size), 1)
    in_panel = (cols >= first) & (cols < first + PANEL)
    for b in range(obs_blocks):
        negative = pivots[pl.ds(b, PANEL, stride=obs_blocks), :]
        whole = moments[pl.ds(b, size, stride=obs_blocks), :]
        rows = pl.ds(first * obs_blocks + b, PANEL, stride=obs_blocks)
        above = moments[rows, :]
        update = jnp.where(in_panel[:PANEL], negative, -dot_nn(negative, whole))
        moments[pl.ds(b, size, stride=obs_blocks), :] = jnp.where(in_panel, 0.0, whole) - dot_tn(above, update)
        moments[rows, :] = update


def kernel(
    members, order, columns, place, values, sigma, operator, gathered,
    analysis, logw, ess,
    states, anomalies, offsets, crosses, moments, pivots, misfits, loglik, sems,
):
    batches, obs_blocks, size = values.shape
    groups, blocks, width, _ = gathered.shape
    mem_count = members // width
    copies = []
    for g in range(groups):
        z, m = g // mem_count, g % mem_count
        copies.append(
            pltpu.make_async_copy(
                gathered.at[g],
                states.at[pl.ds(z * blocks, blocks), pl.ds(m * width, width), :],
                sems.at[g],
            )
        )
    for copy in copies:
        copy.start()
    misfits[...] = jnp.zeros_like(misfits)
    for copy in copies:
        copy.wait()
    eye = (
        lax.broadcasted_iota(jnp.int32, (size, size), 0)
        == lax.broadcasted_iota(jnp.int32, (size, size), 1)
    ).astype(jnp.float32)

    @pl.loop(0, batches)
    def _(step):
        chosen = order[step]
        values_now = values[chosen]
        sigma_now = sigma[chosen]
        for b in range(obs_blocks):
            left = states[columns[chosen, b, 0]]
            right = states[columns[chosen, b, 1]]
            image = dot_nt(left, operator[chosen, b, 0]) + dot_nt(right, operator[chosen, b, 1])
            value = values_now[b : b + 1]
            deviation = sigma_now[b : b + 1]
            misfit = (value - image) / deviation
            misfits[...] += misfit * misfit
            center = jnp.sum(image, axis=0, keepdims=True) / members
            anomaly = image - center
            offsets[b : b + 1, :] = value - center
            anomalies[b] = anomaly
            product = dot_tn(anomaly, jnp.concatenate([left, right, anomaly], axis=1)) / (members - 1)
            crosses[b] = product[:, : 2 * size]
            moments[pl.ds(b, size, stride=obs_blocks), :] = product[:, 2 * size :] + eye * (deviation * deviation)

        @pl.loop(0, size // PANEL)
        def _(panel):
            sweep_panel(moments, pivots, obs_blocks, size, panel)

        for b in range(obs_blocks):
            target = offsets[b : b + 1, :] - 0.5 * anomalies[b]
            weights = -dot_nn(target, moments[pl.ds(b, size, stride=obs_blocks), :])
            change = dot_nn(weights, crosses[b])
            states[columns[chosen, b, 0]] += change[:, :size]
            states[columns[chosen, b, 1]] += change[:, size:]

    temper = 1.0 / math.sqrt(batches * obs_blocks * size)
    likely = -0.5 * temper * jnp.sum(misfits[...], axis=1, keepdims=True)
    largest = jnp.max(likely, axis=0, keepdims=True)
    scaled = jnp.exp(likely - largest)
    summed = jnp.sum(scaled, axis=0, keepdims=True)
    squares = jnp.sum(scaled * scaled, axis=0, keepdims=True)
    loglik[...] = likely - largest - jnp.log(summed)
    ess[...] = summed * summed / squares
    mine = pl.ds(pl.multiple_of(place[0] * width, width), width)
    logw[...] = loglik[mine, :]
    for l in range(blocks):
        analysis[l] = states[place[1] * blocks + l, mine, :]


def gathered_shards(ensemble, obs_values, obs_sigma, obs_operator, block_cols, batch_order):
    size = obs_operator.shape[-1]
    row_count, width = ensemble.shape
    blocks = row_count // size
    mem_count, st_count = lax.axis_size("mem"), lax.axis_size("st")
    members = width * mem_count
    batches, obs_blocks, _ = block_cols.shape
    local = ensemble.reshape(blocks, size, width).transpose(0, 2, 1)
    gathered = lax.all_gather(local, ("st", "mem"))
    place = jnp.stack([lax.axis_index("mem"), lax.axis_index("st")]).astype(jnp.int32)
    smem = pl.BlockSpec(memory_space=pltpu.SMEM)
    vmem = pl.BlockSpec(memory_space=pltpu.VMEM)
    analysis, logw, ess = pl.pallas_call(
        functools.partial(kernel, members),
        out_shape=(
            jax.ShapeDtypeStruct((blocks, width, size), jnp.float32),
            jax.ShapeDtypeStruct((width, 1), jnp.float32),
            jax.ShapeDtypeStruct((1, 1), jnp.float32),
        ),
        in_specs=[smem, smem, smem, vmem, vmem, vmem, pl.BlockSpec(memory_space=pl.ANY)],
        out_specs=(vmem, vmem, vmem),
        scratch_shapes=[
            pltpu.VMEM((st_count * blocks, members, size), jnp.float32),
            pltpu.VMEM((obs_blocks, members, size), jnp.float32),
            pltpu.VMEM((obs_blocks, size), jnp.float32),
            pltpu.VMEM((obs_blocks, size, 2 * size), jnp.float32),
            pltpu.VMEM((size * obs_blocks, size), jnp.float32),
            pltpu.VMEM((PANEL * obs_blocks, size), jnp.float32),
            pltpu.VMEM((members, size), jnp.float32),
            pltpu.VMEM((members, 1), jnp.float32),
            pltpu.SemaphoreType.DMA((mem_count * st_count,)),
        ],
        compiler_params=pltpu.CompilerParams(vmem_limit_bytes=48 << 20),
    )(batch_order, block_cols, place, obs_values, obs_sigma, obs_operator, gathered)
    states = analysis.transpose(0, 2, 1).reshape(row_count, width)
    return states, logw.reshape(width), ess.reshape(())


def solve_blocks(moment, target):
    factor = jnp.linalg.cholesky(moment)
    return jax.vmap(lambda lower, right: jax.scipy.linalg.cho_solve((lower, True), right))(
        factor, target
    )


def reduced_shards(ensemble, obs_values, obs_sigma, obs_operator, block_cols, batch_order):
    block_size = obs_operator.shape[-1]
    row_count, mem_dev = ensemble.shape
    nblocks = row_count // block_size
    members = mem_dev * lax.axis_size("mem")
    batches, obs_blocks, col_count = block_cols.shape
    temper = 1.0 / math.sqrt(batches * obs_blocks * block_size)
    offset = lax.axis_index("st") * nblocks
    states = ensemble.reshape(nblocks, block_size, mem_dev)
    eye = jnp.eye(block_size, dtype=jnp.float32)
    slots = jnp.arange(nblocks, dtype=jnp.int32)
    loglik = jnp.zeros((mem_dev,), jnp.float32)
    for batch_step in range(batches):
        chosen = batch_order[batch_step]
        operator_now = lax.dynamic_index_in_dim(obs_operator, chosen, 0, keepdims=False)
        columns = lax.dynamic_index_in_dim(block_cols, chosen, 0, keepdims=False)
        values_now = lax.dynamic_index_in_dim(obs_values, chosen, 0, keepdims=False)
        sigma_now = lax.dynamic_index_in_dim(obs_sigma, chosen, 0, keepdims=False)
        local_ids = columns.reshape(-1) - offset
        selector = (local_ids[:, None] == slots[None, :]).astype(jnp.float32)
        picked = jnp.einsum("ps,sim->pim", selector, states, precision=precise)
        picked = picked.reshape(obs_blocks, col_count, block_size, mem_dev)
        partial_value = jnp.einsum("bkij,bkjm->bim", operator_now, picked, precision=precise)
        image = lax.psum(partial_value, "st")
        misfit = (values_now[:, :, None] - image) / sigma_now[:, :, None]
        loglik = loglik - 0.5 * temper * jnp.sum(misfit * misfit, axis=(0, 1))
        center = lax.psum(jnp.sum(image, axis=2), "mem") / members
        anomaly = image - center[:, :, None]
        moment_sum, cross_sum = lax.psum(
            (
                jnp.einsum("bim,bjm->bij", anomaly, anomaly, precision=precise),
                jnp.einsum("bkim,bjm->bkij", picked, anomaly, precision=precise),
            ),
            "mem",
        )
        moment = moment_sum / (members - 1) + eye * (sigma_now * sigma_now)[:, :, None]
        cross = cross_sum / (members - 1)
        target = (values_now - center)[:, :, None] - 0.5 * anomaly
        weights = solve_blocks(moment, target)
        change = jnp.einsum("bkij,bjm->bkim", cross, weights, precision=precise)
        change = change.reshape(obs_blocks * col_count, block_size, mem_dev)
        states = states + jnp.einsum("ps,pim->sim", selector, change, precision=precise)
    largest_local = jnp.max(loglik)
    largest = lax.pmax(largest_local, "mem")
    scaled = jnp.exp(loglik - largest)
    summed, squares = lax.psum((jnp.sum(scaled), jnp.sum(scaled * scaled)), "mem")
    log_weights = loglik - largest - jnp.log(summed)
    ess = summed * summed / squares
    return (states.reshape(row_count, mem_dev), log_weights, ess)


def shards(ensemble, *others):
    devices = lax.axis_size("mem") * lax.axis_size("st")
    fits = 4 * ensemble.size * devices <= GATHER_LIMIT
    return (gathered_shards if fits else reduced_shards)(ensemble, *others)


def solution(mesh):
    placed = (P("st", "mem"), P(), P(), P(), P(), P())
    return jax.shard_map(
        shards,
        mesh=mesh,
        in_specs=placed,
        out_specs=(P("st", "mem"), P("mem"), P()),
        check_vma=False,
    )
```

```python
import functools
import math

import jax
import jax.numpy as jnp
from jax import lax
from jax.experimental import pallas as pl
from jax.experimental.pallas import tpu as pltpu
from jax.sharding import PartitionSpec as P

precise = lax.Precision.HIGHEST
PANEL = 16
GATHER_LIMIT = 16 << 20


def dot_nt(a, b):
    return lax.dot_general(a, b, (((1,), (1,)), ((), ())), precision=precise, preferred_element_type=jnp.float32)


def dot_tn(a, b):
    return lax.dot_general(a, b, (((0,), (0,)), ((), ())), precision=precise, preferred_element_type=jnp.float32)


def dot_nn(a, b):
    return lax.dot_general(a, b, (((1,), (0,)), ((), ())), precision=precise, preferred_element_type=jnp.float32)


def sweep_panel(moments, pivots, obs_blocks, size, panel):
    first = panel * PANEL
    lanes = lax.broadcasted_iota(jnp.int32, (obs_blocks, size), 1)
    inside = (lanes >= first) & (lanes < first + PANEL)
    entry, rows = {}, []
    for i in range(PANEL):
        row = moments[pl.ds(first + i, obs_blocks, stride=size), :]
        rows.append(row)
        row = pltpu.roll(row, size - first, 1)
        for j in range(i + 1):
            entry[i, j] = jnp.broadcast_to(row[:, j : j + 1], (obs_blocks, size))

    def at(i, j):
        return (i, j) if i >= j else (j, i)

    for p in range(PANEL):
        inverse = 1.0 / entry[p, p]
        column = {i: entry[at(i, p)] for i in range(PANEL) if i != p}
        scaled = {i: column[i] * inverse for i in column}
        for i in column:
            for j in column:
                if j <= i:
                    entry[i, j] = entry[i, j] - scaled[i] * column[j]
        for i in column:
            entry[at(i, p)] = scaled[i]
        entry[p, p] = -inverse
    for i in range(PANEL):
        placed = jnp.zeros((obs_blocks, size), jnp.float32)
        total = jnp.zeros((obs_blocks, size), jnp.float32)
        for j in range(PANEL):
            placed = jnp.where(lanes == first + j, entry[at(i, j)], placed)
            total = total - entry[at(i, j)] * rows[j]
        pivots[pl.ds(i, obs_blocks, stride=PANEL), :] = jnp.where(inside, placed, total)

    cols = lax.broadcasted_iota(jnp.int32, (size, size), 1)
    in_panel = (cols >= first) & (cols < first + PANEL)
    swept = []
    for b in range(obs_blocks):
        start = pl.multiple_of(b * size + first, PANEL)
        update = pivots[b * PANEL : (b + 1) * PANEL, :]
        whole = moments[b * size : (b + 1) * size, :]
        above = moments[pl.ds(start, PANEL), :]
        swept.append(jnp.where(in_panel, 0.0, whole) - dot_tn(above, update))
    for b in range(obs_blocks):
        moments[b * size : (b + 1) * size, :] = swept[b]
    for b in range(obs_blocks):
        start = pl.multiple_of(b * size + first, PANEL)
        moments[pl.ds(start, PANEL), :] = pivots[b * PANEL : (b + 1) * PANEL, :]


def kernel(
    members, order, columns, place, values, sigma, operator, gathered,
    analysis, logw, ess,
    states, anomalies, offsets, crosses, moments, pivots, misfits, loglik, sems,
):
    batches, obs_blocks, size = values.shape
    groups, blocks, width, _ = gathered.shape
    mem_count = members // width
    copies = []
    for g in range(groups):
        z, m = g // mem_count, g % mem_count
        copies.append(
            pltpu.make_async_copy(
                gathered.at[g],
                states.at[pl.ds(z * blocks, blocks), pl.ds(m * width, width), :],
                sems.at[g],
            )
        )
    for copy in copies:
        copy.start()
    misfits[...] = jnp.zeros_like(misfits)
    for copy in copies:
        copy.wait()
    eye = (
        lax.broadcasted_iota(jnp.int32, (size, size), 0)
        == lax.broadcasted_iota(jnp.int32, (size, size), 1)
    ).astype(jnp.float32)

    @pl.loop(0, batches)
    def _(step):
        chosen = order[step]
        values_now = values[chosen]
        sigma_now = sigma[chosen]
        for b in range(obs_blocks):
            left = states[columns[chosen, b, 0]]
            right = states[columns[chosen, b, 1]]
            image = dot_nt(left, operator[chosen, b, 0]) + dot_nt(right, operator[chosen, b, 1])
            value = values_now[b : b + 1]
            deviation = sigma_now[b : b + 1]
            misfit = (value - image) / deviation
            misfits[...] += misfit * misfit
            center = jnp.sum(image, axis=0, keepdims=True) / members
            anomaly = image - center
            offsets[b : b + 1, :] = value - center
            anomalies[b] = anomaly
            product = dot_tn(anomaly, jnp.concatenate([left, right, anomaly], axis=1)) / (members - 1)
            crosses[b] = product[:, : 2 * size]
            moments[b * size : (b + 1) * size, :] = product[:, 2 * size :] + eye * (deviation * deviation)

        @pl.loop(0, size // PANEL)
        def _(panel):
            sweep_panel(moments, pivots, obs_blocks, size, panel)

        for b in range(obs_blocks):
            target = offsets[b : b + 1, :] - 0.5 * anomalies[b]
            weights = -dot_nn(target, moments[b * size : (b + 1) * size, :])
            change = dot_nn(weights, crosses[b])
            states[columns[chosen, b, 0]] += change[:, :size]
            states[columns[chosen, b, 1]] += change[:, size:]

    temper = 1.0 / math.sqrt(batches * obs_blocks * size)
    likely = -0.5 * temper * jnp.sum(misfits[...], axis=1, keepdims=True)
    largest = jnp.max(likely, axis=0, keepdims=True)
    scaled = jnp.exp(likely - largest)
    summed = jnp.sum(scaled, axis=0, keepdims=True)
    squares = jnp.sum(scaled * scaled, axis=0, keepdims=True)
    loglik[...] = likely - largest - jnp.log(summed)
    ess[...] = summed * summed / squares
    mine = pl.ds(pl.multiple_of(place[0] * width, width), width)
    logw[...] = loglik[mine, :]
    for l in range(blocks):
        analysis[l] = states[place[1] * blocks + l, mine, :]


def gathered_shards(ensemble, obs_values, obs_sigma, obs_operator, block_cols, batch_order):
    size = obs_operator.shape[-1]
    row_count, width = ensemble.shape
    blocks = row_count // size
    mem_count, st_count = lax.axis_size("mem"), lax.axis_size("st")
    members = width * mem_count
    batches, obs_blocks, _ = block_cols.shape
    local = ensemble.reshape(blocks, size, width).transpose(0, 2, 1)
    gathered = lax.all_gather(local, ("st", "mem"))
    place = jnp.stack([lax.axis_index("mem"), lax.axis_index("st")]).astype(jnp.int32)
    smem = pl.BlockSpec(memory_space=pltpu.SMEM)
    vmem = pl.BlockSpec(memory_space=pltpu.VMEM)
    analysis, logw, ess = pl.pallas_call(
        functools.partial(kernel, members),
        out_shape=(
            jax.ShapeDtypeStruct((blocks, width, size), jnp.float32),
            jax.ShapeDtypeStruct((width, 1), jnp.float32),
            jax.ShapeDtypeStruct((1, 1), jnp.float32),
        ),
        in_specs=[smem, smem, smem, vmem, vmem, vmem, pl.BlockSpec(memory_space=pl.ANY)],
        out_specs=(vmem, vmem, vmem),
        scratch_shapes=[
            pltpu.VMEM((st_count * blocks, members, size), jnp.float32),
            pltpu.VMEM((obs_blocks, members, size), jnp.float32),
            pltpu.VMEM((obs_blocks, size), jnp.float32),
            pltpu.VMEM((obs_blocks, size, 2 * size), jnp.float32),
            pltpu.VMEM((size * obs_blocks, size), jnp.float32),
            pltpu.VMEM((PANEL * obs_blocks, size), jnp.float32),
            pltpu.VMEM((members, size), jnp.float32),
            pltpu.VMEM((members, 1), jnp.float32),
            pltpu.SemaphoreType.DMA((mem_count * st_count,)),
        ],
        compiler_params=pltpu.CompilerParams(vmem_limit_bytes=48 << 20),
    )(batch_order, block_cols, place, obs_values, obs_sigma, obs_operator, gathered)
    states = analysis.transpose(0, 2, 1).reshape(row_count, width)
    return states, logw.reshape(width), ess.reshape(())


def solve_blocks(moment, target):
    factor = jnp.linalg.cholesky(moment)
    return jax.vmap(lambda lower, right: jax.scipy.linalg.cho_solve((lower, True), right))(
        factor, target
    )


def reduced_shards(ensemble, obs_values, obs_sigma, obs_operator, block_cols, batch_order):
    block_size = obs_operator.shape[-1]
    row_count, mem_dev = ensemble.shape
    nblocks = row_count // block_size
    members = mem_dev * lax.axis_size("mem")
    batches, obs_blocks, col_count = block_cols.shape
    temper = 1.0 / math.sqrt(batches * obs_blocks * block_size)
    offset = lax.axis_index("st") * nblocks
    states = ensemble.reshape(nblocks, block_size, mem_dev)
    eye = jnp.eye(block_size, dtype=jnp.float32)
    slots = jnp.arange(nblocks, dtype=jnp.int32)
    loglik = jnp.zeros((mem_dev,), jnp.float32)
    for batch_step in range(batches):
        chosen = batch_order[batch_step]
        operator_now = lax.dynamic_index_in_dim(obs_operator, chosen, 0, keepdims=False)
        columns = lax.dynamic_index_in_dim(block_cols, chosen, 0, keepdims=False)
        values_now = lax.dynamic_index_in_dim(obs_values, chosen, 0, keepdims=False)
        sigma_now = lax.dynamic_index_in_dim(obs_sigma, chosen, 0, keepdims=False)
        local_ids = columns.reshape(-1) - offset
        selector = (local_ids[:, None] == slots[None, :]).astype(jnp.float32)
        picked = jnp.einsum("ps,sim->pim", selector, states, precision=precise)
        picked = picked.reshape(obs_blocks, col_count, block_size, mem_dev)
        partial_value = jnp.einsum("bkij,bkjm->bim", operator_now, picked, precision=precise)
        image = lax.psum(partial_value, "st")
        misfit = (values_now[:, :, None] - image) / sigma_now[:, :, None]
        loglik = loglik - 0.5 * temper * jnp.sum(misfit * misfit, axis=(0, 1))
        center = lax.psum(jnp.sum(image, axis=2), "mem") / members
        anomaly = image - center[:, :, None]
        moment_sum, cross_sum = lax.psum(
            (
                jnp.einsum("bim,bjm->bij", anomaly, anomaly, precision=precise),
                jnp.einsum("bkim,bjm->bkij", picked, anomaly, precision=precise),
            ),
            "mem",
        )
        moment = moment_sum / (members - 1) + eye * (sigma_now * sigma_now)[:, :, None]
        cross = cross_sum / (members - 1)
        target = (values_now - center)[:, :, None] - 0.5 * anomaly
        weights = solve_blocks(moment, target)
        change = jnp.einsum("bkij,bjm->bkim", cross, weights, precision=precise)
        change = change.reshape(obs_blocks * col_count, block_size, mem_dev)
        states = states + jnp.einsum("ps,pim->sim", selector, change, precision=precise)
    largest_local = jnp.max(loglik)
    largest = lax.pmax(largest_local, "mem")
    scaled = jnp.exp(loglik - largest)
    summed, squares = lax.psum((jnp.sum(scaled), jnp.sum(scaled * scaled)), "mem")
    log_weights = loglik - largest - jnp.log(summed)
    ess = summed * summed / squares
    return (states.reshape(row_count, mem_dev), log_weights, ess)


def shards(ensemble, *others):
    devices = lax.axis_size("mem") * lax.axis_size("st")
    fits = 4 * ensemble.size * devices <= GATHER_LIMIT
    return (gathered_shards if fits else reduced_shards)(ensemble, *others)


def solution(mesh):
    placed = (P("st", "mem"), P(), P(), P(), P(), P())
    return jax.shard_map(
        shards,
        mesh=mesh,
        in_specs=placed,
        out_specs=(P("st", "mem"), P("mem"), P()),
        check_vma=False,
    )
```

```python
import functools
import math

import jax
import jax.numpy as jnp
from jax import lax
from jax.experimental import pallas as pl
from jax.experimental.pallas import tpu as pltpu
from jax.sharding import PartitionSpec as P

precise = lax.Precision.HIGHEST
PANEL = 16
GATHER_LIMIT = 16 << 20


def dot_nt(a, b):
    return lax.dot_general(a, b, (((1,), (1,)), ((), ())), precision=precise, preferred_element_type=jnp.float32)


def dot_tn(a, b):
    return lax.dot_general(a, b, (((0,), (0,)), ((), ())), precision=precise, preferred_element_type=jnp.float32)


def dot_nn(a, b):
    return lax.dot_general(a, b, (((1,), (0,)), ((), ())), precision=precise, preferred_element_type=jnp.float32)


def sweep_panel(moments, pivots, obs_blocks, size, panel):
    first = panel * PANEL
    lanes = lax.broadcasted_iota(jnp.int32, (obs_blocks, size), 1)
    inside = (lanes >= first) & (lanes < first + PANEL)
    entry, rows = {}, []
    for i in range(PANEL):
        row = moments[pl.ds(first + i, obs_blocks, stride=size), :]
        rows.append(row)
        row = pltpu.roll(row, size - first, 1)
        for j in range(i + 1):
            entry[i, j] = jnp.broadcast_to(row[:, j : j + 1], (obs_blocks, size))

    def at(i, j):
        return (i, j) if i >= j else (j, i)

    for p in range(PANEL):
        inverse = 1.0 / entry[p, p]
        column = {i: entry[at(i, p)] for i in range(PANEL) if i != p}
        scaled = {i: column[i] * inverse for i in column}
        for i in column:
            for j in column:
                if j <= i:
                    entry[i, j] = entry[i, j] - scaled[i] * column[j]
        for i in column:
            entry[at(i, p)] = scaled[i]
        entry[p, p] = -inverse
    for i in range(PANEL):
        placed = jnp.zeros((obs_blocks, size), jnp.float32)
        total = jnp.zeros((obs_blocks, size), jnp.float32)
        for j in range(PANEL):
            placed = jnp.where(lanes == first + j, entry[at(i, j)], placed)
            total = total - entry[at(i, j)] * rows[j]
        pivots[pl.ds(i, obs_blocks, stride=PANEL), :] = jnp.where(inside, placed, total)

    cols = lax.broadcasted_iota(jnp.int32, (size, size), 1)
    in_panel = (cols >= first) & (cols < first + PANEL)
    swept = []
    for b in range(obs_blocks):
        start = pl.multiple_of(b * size + first, PANEL)
        update = pivots[b * PANEL : (b + 1) * PANEL, :]
        whole = moments[b * size : (b + 1) * size, :]
        above = moments[pl.ds(start, PANEL), :]
        swept.append(jnp.where(in_panel, 0.0, whole) - dot_tn(above, update))
    for b in range(obs_blocks):
        moments[b * size : (b + 1) * size, :] = swept[b]
    for b in range(obs_blocks):
        start = pl.multiple_of(b * size + first, PANEL)
        moments[pl.ds(start, PANEL), :] = pivots[b * PANEL : (b + 1) * PANEL, :]


def kernel(
    members, order, columns, place, values, sigma, operator, gathered,
    analysis, logw, ess,
    states, anomalies, offsets, crosses, moments, pivots, misfits, loglik, sems,
):
    batches, obs_blocks, size = values.shape
    groups, blocks, width, _ = gathered.shape
    mem_count = members // width
    copies = []
    for g in range(groups):
        z, m = g // mem_count, g % mem_count
        copies.append(
            pltpu.make_async_copy(
                gathered.at[g],
                states.at[pl.ds(z * blocks, blocks), pl.ds(m * width, width), :],
                sems.at[g],
            )
        )
    for copy in copies:
        copy.start()
    misfits[...] = jnp.zeros_like(misfits)
    for copy in copies:
        copy.wait()
    eye = (
        lax.broadcasted_iota(jnp.int32, (size, size), 0)
        == lax.broadcasted_iota(jnp.int32, (size, size), 1)
    ).astype(jnp.float32)

    @pl.loop(0, batches)
    def _(step):
        chosen = order[step]
        values_now = values[chosen]
        sigma_now = sigma[chosen]
        for b in range(obs_blocks):
            left = states[columns[chosen, b, 0]]
            right = states[columns[chosen, b, 1]]
            image = dot_nt(left, operator[chosen, b, 0]) + dot_nt(right, operator[chosen, b, 1])
            value = values_now[b : b + 1]
            deviation = sigma_now[b : b + 1]
            misfit = (value - image) / deviation
            misfits[...] += misfit * misfit
            center = jnp.sum(image, axis=0, keepdims=True) / members
            anomaly = image - center
            offsets[b : b + 1, :] = value - center
            anomalies[b] = anomaly
            product = dot_tn(anomaly, jnp.concatenate([left, right, anomaly], axis=1)) / (members - 1)
            crosses[b] = product[:, : 2 * size]
            moments[b * size : (b + 1) * size, :] = product[:, 2 * size :] + eye * (deviation * deviation)

        @pl.loop(0, size // PANEL)
        def _(panel):
            sweep_panel(moments, pivots, obs_blocks, size, panel)

        for b in range(obs_blocks):
            target = offsets[b : b + 1, :] - 0.5 * anomalies[b]
            weights = -dot_nn(target, moments[b * size : (b + 1) * size, :])
            change = dot_nn(weights, crosses[b])
            states[columns[chosen, b, 0]] += change[:, :size]
            states[columns[chosen, b, 1]] += change[:, size:]

    temper = 1.0 / math.sqrt(batches * obs_blocks * size)
    likely = -0.5 * temper * jnp.sum(misfits[...], axis=1, keepdims=True)
    largest = jnp.max(likely, axis=0, keepdims=True)
    scaled = jnp.exp(likely - largest)
    summed = jnp.sum(scaled, axis=0, keepdims=True)
    squares = jnp.sum(scaled * scaled, axis=0, keepdims=True)
    loglik[...] = likely - largest - jnp.log(summed)
    ess[...] = summed * summed / squares
    mine = pl.ds(pl.multiple_of(place[0] * width, width), width)
    logw[...] = loglik[mine, :]
    for l in range(blocks):
        analysis[l] = states[place[1] * blocks + l, mine, :]


MESH = pl.DeviceIdType.MESH


def gather_kernel(piece, gathered, send_sems, recv_sems, local_sem):
    me, z = lax.axis_index("mem"), lax.axis_index("st")
    depth, width = lax.axis_size("st"), lax.axis_size("mem")
    core, bit = me % 2, (me // 2) % 2
    twin = me + 1 - 2 * core
    flat = me + 2 - 4 * bit
    upright = (me + width // 2) % width
    corner = (flat + width // 2) % width
    kinds = {"up": 0, "down": 1, "flat": 2, "upright": 3, "twin": 4}
    targets = {"up": (me, z + 1), "down": (me, z - 1), "flat": (flat, z), "upright": (upright, z), "twin": (twin, z)}

    def copy(kind, slot, source=None):
        return pltpu.make_async_remote_copy(
            src_ref=gathered.at[slot] if source is None else source,
            dst_ref=gathered.at[slot],
            send_sem=send_sems.at[kinds[kind] * depth * width + slot],
            recv_sem=recv_sems.at[slot],
            device_id=targets[kind],
            device_id_type=MESH,
        )

    def arrive(slot):
        copy("twin", slot).wait_recv()

    barrier = pltpu.get_barrier_semaphore()
    for kind in ("flat", "upright", "twin"):
        pl.semaphore_signal(barrier, inc=1, device_id=targets[kind], device_id_type=MESH)

    @pl.when(z < depth - 1)
    def _():
        pl.semaphore_signal(barrier, inc=1, device_id=targets["up"], device_id_type=MESH)

    @pl.when(z > 0)
    def _():
        pl.semaphore_signal(barrier, inc=1, device_id=targets["down"], device_id_type=MESH)

    @pl.when((z > 0) & (z < depth - 1))
    def _():
        pl.semaphore_wait(barrier, 5)

    @pl.when((z == 0) | (z == depth - 1))
    def _():
        pl.semaphore_wait(barrier, 4)

    def column(action, level, distance, rising):
        slot = level * width + me
        source = piece if distance == 0 else None
        if distance == 0 or rising:
            @pl.when(z < depth - 1)
            def _():
                action(copy("up", slot, source))

        if distance == 0 or not rising:
            @pl.when(z > 0)
            def _():
                action(copy("down", slot, source))

        for kind in ("flat", "upright", "twin"):
            action(copy(kind, slot, source))

    def plane(action, level, wait):
        for first, onward, parity in ((flat, "upright", 1), (upright, "flat", 0)):
            slot = level * width + first
            if wait:
                arrive(slot)

            @pl.when(level % 2 == parity)
            def _():
                action(copy(onward, slot))

            action(copy("twin", slot))

    def far(action, level, wait):
        slot = level * width + corner
        if wait:
            arrive(slot)
        action(copy("twin", slot))

    def around(distance, do):
        if distance == 0:
            do(z, True)
            return

        @pl.when(z >= distance)
        def _():
            do(z - distance, True)

        @pl.when(z + distance < depth)
        def _():
            do(z + distance, False)

    def start(descriptor):
        descriptor.start()

    def finish(descriptor):
        descriptor.wait_send()

    own = pltpu.make_async_copy(piece, gathered.at[z * width + me], local_sem)
    own.start()
    column(start, z, 0, True)

    for turn in range(1, depth + 2):
        if turn < depth:
            def onward(level, rising, turn=turn):
                arrive(level * width + me)
                column(start, level, turn, rising)
            around(turn, onward)
        if turn - 1 < depth:
            around(turn - 1, lambda level, rising: plane(start, level, True))
        if turn >= 2:
            around(turn - 2, lambda level, rising: far(start, level, True))
    for distance in range(depth):
        def rest(level, rising, distance=distance):
            for other in (twin, flat + twin - me, upright + twin - me, corner + twin - me):
                arrive(level * width + other)
            column(finish, level, distance, rising)
            plane(finish, level, False)
            far(finish, level, False)
        around(distance, rest)
    own.wait()


def gather_all(piece):
    depth, width = lax.axis_size("st"), lax.axis_size("mem")
    if width != 8 or depth < 2:
        return lax.all_gather(piece, ("st", "mem"))
    anywhere = pl.BlockSpec(memory_space=pl.ANY)
    return pl.pallas_call(
        gather_kernel,
        out_shape=jax.ShapeDtypeStruct((depth * width, *piece.shape), piece.dtype),
        in_specs=[anywhere],
        out_specs=anywhere,
        scratch_shapes=[
            pltpu.SemaphoreType.DMA((5 * depth * width,)),
            pltpu.SemaphoreType.DMA((depth * width,)),
            pltpu.SemaphoreType.DMA,
        ],
        compiler_params=pltpu.CompilerParams(collective_id=0, has_side_effects=True),
    )(piece)


def gathered_shards(ensemble, obs_values, obs_sigma, obs_operator, block_cols, batch_order):
    size = obs_operator.shape[-1]
    row_count, width = ensemble.shape
    blocks = row_count // size
    mem_count, st_count = lax.axis_size("mem"), lax.axis_size("st")
    members = width * mem_count
    batches, obs_blocks, _ = block_cols.shape
    local = ensemble.reshape(blocks, size, width).transpose(0, 2, 1)
    gathered = gather_all(local)
    place = jnp.stack([lax.axis_index("mem"), lax.axis_index("st")]).astype(jnp.int32)
    smem = pl.BlockSpec(memory_space=pltpu.SMEM)
    vmem = pl.BlockSpec(memory_space=pltpu.VMEM)
    analysis, logw, ess = pl.pallas_call(
        functools.partial(kernel, members),
        out_shape=(
            jax.ShapeDtypeStruct((blocks, width, size), jnp.float32),
            jax.ShapeDtypeStruct((width, 1), jnp.float32),
            jax.ShapeDtypeStruct((1, 1), jnp.float32),
        ),
        in_specs=[smem, smem, smem, vmem, vmem, vmem, pl.BlockSpec(memory_space=pl.ANY)],
        out_specs=(vmem, vmem, vmem),
        scratch_shapes=[
            pltpu.VMEM((st_count * blocks, members, size), jnp.float32),
            pltpu.VMEM((obs_blocks, members, size), jnp.float32),
            pltpu.VMEM((obs_blocks, size), jnp.float32),
            pltpu.VMEM((obs_blocks, size, 2 * size), jnp.float32),
            pltpu.VMEM((size * obs_blocks, size), jnp.float32),
            pltpu.VMEM((PANEL * obs_blocks, size), jnp.float32),
            pltpu.VMEM((members, size), jnp.float32),
            pltpu.VMEM((members, 1), jnp.float32),
            pltpu.SemaphoreType.DMA((mem_count * st_count,)),
        ],
        compiler_params=pltpu.CompilerParams(vmem_limit_bytes=48 << 20),
    )(batch_order, block_cols, place, obs_values, obs_sigma, obs_operator, gathered)
    states = analysis.transpose(0, 2, 1).reshape(row_count, width)
    return states, logw.reshape(width), ess.reshape(())


def solve_blocks(moment, target):
    factor = jnp.linalg.cholesky(moment)
    return jax.vmap(lambda lower, right: jax.scipy.linalg.cho_solve((lower, True), right))(
        factor, target
    )


def reduced_shards(ensemble, obs_values, obs_sigma, obs_operator, block_cols, batch_order):
    block_size = obs_operator.shape[-1]
    row_count, mem_dev = ensemble.shape
    nblocks = row_count // block_size
    members = mem_dev * lax.axis_size("mem")
    batches, obs_blocks, col_count = block_cols.shape
    temper = 1.0 / math.sqrt(batches * obs_blocks * block_size)
    offset = lax.axis_index("st") * nblocks
    states = ensemble.reshape(nblocks, block_size, mem_dev)
    eye = jnp.eye(block_size, dtype=jnp.float32)
    slots = jnp.arange(nblocks, dtype=jnp.int32)
    loglik = jnp.zeros((mem_dev,), jnp.float32)
    for batch_step in range(batches):
        chosen = batch_order[batch_step]
        operator_now = lax.dynamic_index_in_dim(obs_operator, chosen, 0, keepdims=False)
        columns = lax.dynamic_index_in_dim(block_cols, chosen, 0, keepdims=False)
        values_now = lax.dynamic_index_in_dim(obs_values, chosen, 0, keepdims=False)
        sigma_now = lax.dynamic_index_in_dim(obs_sigma, chosen, 0, keepdims=False)
        local_ids = columns.reshape(-1) - offset
        selector = (local_ids[:, None] == slots[None, :]).astype(jnp.float32)
        picked = jnp.einsum("ps,sim->pim", selector, states, precision=precise)
        picked = picked.reshape(obs_blocks, col_count, block_size, mem_dev)
        partial_value = jnp.einsum("bkij,bkjm->bim", operator_now, picked, precision=precise)
        image = lax.psum(partial_value, "st")
        misfit = (values_now[:, :, None] - image) / sigma_now[:, :, None]
        loglik = loglik - 0.5 * temper * jnp.sum(misfit * misfit, axis=(0, 1))
        center = lax.psum(jnp.sum(image, axis=2), "mem") / members
        anomaly = image - center[:, :, None]
        moment_sum, cross_sum = lax.psum(
            (
                jnp.einsum("bim,bjm->bij", anomaly, anomaly, precision=precise),
                jnp.einsum("bkim,bjm->bkij", picked, anomaly, precision=precise),
            ),
            "mem",
        )
        moment = moment_sum / (members - 1) + eye * (sigma_now * sigma_now)[:, :, None]
        cross = cross_sum / (members - 1)
        target = (values_now - center)[:, :, None] - 0.5 * anomaly
        weights = solve_blocks(moment, target)
        change = jnp.einsum("bkij,bjm->bkim", cross, weights, precision=precise)
        change = change.reshape(obs_blocks * col_count, block_size, mem_dev)
        states = states + jnp.einsum("ps,pim->sim", selector, change, precision=precise)
    largest_local = jnp.max(loglik)
    largest = lax.pmax(largest_local, "mem")
    scaled = jnp.exp(loglik - largest)
    summed, squares = lax.psum((jnp.sum(scaled), jnp.sum(scaled * scaled)), "mem")
    log_weights = loglik - largest - jnp.log(summed)
    ess = summed * summed / squares
    return (states.reshape(row_count, mem_dev), log_weights, ess)


def shards(ensemble, *others):
    devices = lax.axis_size("mem") * lax.axis_size("st")
    fits = 4 * ensemble.size * devices <= GATHER_LIMIT
    return (gathered_shards if fits else reduced_shards)(ensemble, *others)


def solution(mesh):
    placed = (P("st", "mem"), P(), P(), P(), P(), P())
    return jax.shard_map(
        shards,
        mesh=mesh,
        in_specs=placed,
        out_specs=(P("st", "mem"), P("mem"), P()),
        check_vma=False,
    )
```

```python
import functools
import math

import jax
import jax.numpy as jnp
from jax import lax
from jax.experimental import pallas as pl
from jax.experimental.pallas import tpu as pltpu
from jax.sharding import PartitionSpec as P

precise = lax.Precision.HIGHEST
PANEL = 16
GATHER_LIMIT = 16 << 20


def dot_nt(a, b):
    return lax.dot_general(a, b, (((1,), (1,)), ((), ())), precision=precise, preferred_element_type=jnp.float32)


def dot_tn(a, b):
    return lax.dot_general(a, b, (((0,), (0,)), ((), ())), precision=precise, preferred_element_type=jnp.float32)


def dot_nn(a, b):
    return lax.dot_general(a, b, (((1,), (0,)), ((), ())), precision=precise, preferred_element_type=jnp.float32)


def sweep_panel(moments, pivots, obs_blocks, size, panel):
    first = panel * PANEL
    lanes = lax.broadcasted_iota(jnp.int32, (obs_blocks, size), 1)
    inside = (lanes >= first) & (lanes < first + PANEL)
    entry, rows = {}, []
    for i in range(PANEL):
        row = moments[pl.ds(first + i, obs_blocks, stride=size), :]
        rows.append(row)
        row = pltpu.roll(row, size - first, 1)
        for j in range(i + 1):
            entry[i, j] = jnp.broadcast_to(row[:, j : j + 1], (obs_blocks, size))

    def at(i, j):
        return (i, j) if i >= j else (j, i)

    for p in range(PANEL):
        inverse = 1.0 / entry[p, p]
        column = {i: entry[at(i, p)] for i in range(PANEL) if i != p}
        scaled = {i: column[i] * inverse for i in column}
        for i in column:
            for j in column:
                if j <= i:
                    entry[i, j] = entry[i, j] - scaled[i] * column[j]
        for i in column:
            entry[at(i, p)] = scaled[i]
        entry[p, p] = -inverse
    for i in range(PANEL):
        placed = jnp.zeros((obs_blocks, size), jnp.float32)
        total = jnp.zeros((obs_blocks, size), jnp.float32)
        for j in range(PANEL):
            placed = jnp.where(lanes == first + j, entry[at(i, j)], placed)
            total = total - entry[at(i, j)] * rows[j]
        pivots[pl.ds(i, obs_blocks, stride=PANEL), :] = jnp.where(inside, placed, total)

    cols = lax.broadcasted_iota(jnp.int32, (size, size), 1)
    in_panel = (cols >= first) & (cols < first + PANEL)
    swept = []
    for b in range(obs_blocks):
        start = pl.multiple_of(b * size + first, PANEL)
        update = pivots[b * PANEL : (b + 1) * PANEL, :]
        whole = moments[b * size : (b + 1) * size, :]
        above = moments[pl.ds(start, PANEL), :]
        swept.append(jnp.where(in_panel, 0.0, whole) - dot_tn(above, update))
    for b in range(obs_blocks):
        moments[b * size : (b + 1) * size, :] = swept[b]
    for b in range(obs_blocks):
        start = pl.multiple_of(b * size + first, PANEL)
        moments[pl.ds(start, PANEL), :] = pivots[b * PANEL : (b + 1) * PANEL, :]


def kernel(
    members, order, columns, place, values, sigma, operator, gathered,
    analysis, logw, ess,
    states, anomalies, offsets, crosses, moments, pivots, misfits, loglik, sems,
):
    batches, obs_blocks, size = values.shape
    groups, blocks, width, _ = gathered.shape
    mem_count = members // width
    copies = []
    for g in range(groups):
        z, m = g // mem_count, g % mem_count
        copies.append(
            pltpu.make_async_copy(
                gathered.at[g],
                states.at[pl.ds(z * blocks, blocks), pl.ds(m * width, width), :],
                sems.at[g],
            )
        )
    for copy in copies:
        copy.start()
    misfits[...] = jnp.zeros_like(misfits)
    for copy in copies:
        copy.wait()
    eye = (
        lax.broadcasted_iota(jnp.int32, (size, size), 0)
        == lax.broadcasted_iota(jnp.int32, (size, size), 1)
    ).astype(jnp.float32)

    @pl.loop(0, batches)
    def _(step):
        chosen = order[step]
        values_now = values[chosen]
        sigma_now = sigma[chosen]
        for b in range(obs_blocks):
            left = states[columns[chosen, b, 0]]
            right = states[columns[chosen, b, 1]]
            both = jnp.concatenate([left, right], axis=1)
            rows = jnp.concatenate([operator[chosen, b, 0], operator[chosen, b, 1]], axis=1)
            image = dot_nt(both, rows)
            value = values_now[b : b + 1]
            deviation = sigma_now[b : b + 1]
            misfit = (value - image) * (1.0 / deviation)
            misfits[...] += misfit * misfit
            center = jnp.sum(image, axis=0, keepdims=True) / members
            anomaly = image - center
            offsets[b : b + 1, :] = value - center
            anomalies[b] = anomaly
            product = dot_tn(anomaly, jnp.concatenate([both, anomaly], axis=1)) * (1.0 / (members - 1))
            crosses[b] = product[:, : 2 * size]
            moments[b * size : (b + 1) * size, :] = product[:, 2 * size :] + eye * (deviation * deviation)

        @pl.loop(0, size // PANEL)
        def _(panel):
            sweep_panel(moments, pivots, obs_blocks, size, panel)

        for b in range(obs_blocks):
            target = offsets[b : b + 1, :] - 0.5 * anomalies[b]
            weights = -dot_nn(target, moments[b * size : (b + 1) * size, :])
            change = dot_nn(weights, crosses[b])
            states[columns[chosen, b, 0]] += change[:, :size]
            states[columns[chosen, b, 1]] += change[:, size:]

    temper = 1.0 / math.sqrt(batches * obs_blocks * size)
    likely = -0.5 * temper * jnp.sum(misfits[...], axis=1, keepdims=True)
    largest = jnp.max(likely, axis=0, keepdims=True)
    scaled = jnp.exp(likely - largest)
    summed = jnp.sum(scaled, axis=0, keepdims=True)
    squares = jnp.sum(scaled * scaled, axis=0, keepdims=True)
    loglik[...] = likely - largest - jnp.log(summed)
    ess[...] = summed * summed / squares
    mine = pl.ds(pl.multiple_of(place[0] * width, width), width)
    logw[...] = loglik[mine, :]
    for l in range(blocks):
        analysis[l] = states[place[1] * blocks + l, mine, :]


MESH = pl.DeviceIdType.MESH


def gather_kernel(piece, gathered, send_sems, recv_sems, local_sem):
    me, z = lax.axis_index("mem"), lax.axis_index("st")
    depth, width = lax.axis_size("st"), lax.axis_size("mem")
    core, bit = me % 2, (me // 2) % 2
    twin = me + 1 - 2 * core
    flat = me + 2 - 4 * bit
    upright = (me + width // 2) % width
    corner = (flat + width // 2) % width
    kinds = {"up": 0, "down": 1, "flat": 2, "upright": 3, "twin": 4}
    targets = {"up": (me, z + 1), "down": (me, z - 1), "flat": (flat, z), "upright": (upright, z), "twin": (twin, z)}

    def copy(kind, slot, source=None):
        return pltpu.make_async_remote_copy(
            src_ref=gathered.at[slot] if source is None else source,
            dst_ref=gathered.at[slot],
            send_sem=send_sems.at[kinds[kind] * depth * width + slot],
            recv_sem=recv_sems.at[slot],
            device_id=targets[kind],
            device_id_type=MESH,
        )

    def arrive(slot):
        copy("twin", slot).wait_recv()

    barrier = pltpu.get_barrier_semaphore()
    for kind in ("flat", "upright", "twin"):
        pl.semaphore_signal(barrier, inc=1, device_id=targets[kind], device_id_type=MESH)

    @pl.when(z < depth - 1)
    def _():
        pl.semaphore_signal(barrier, inc=1, device_id=targets["up"], device_id_type=MESH)

    @pl.when(z > 0)
    def _():
        pl.semaphore_signal(barrier, inc=1, device_id=targets["down"], device_id_type=MESH)

    @pl.when((z > 0) & (z < depth - 1))
    def _():
        pl.semaphore_wait(barrier, 5)

    @pl.when((z == 0) | (z == depth - 1))
    def _():
        pl.semaphore_wait(barrier, 4)

    def column(action, level, distance, rising):
        slot = level * width + me
        source = piece if distance == 0 else None
        if distance == 0 or rising:
            @pl.when(z < depth - 1)
            def _():
                action(copy("up", slot, source))

        if distance == 0 or not rising:
            @pl.when(z > 0)
            def _():
                action(copy("down", slot, source))

        for kind in ("flat", "upright", "twin"):
            action(copy(kind, slot, source))

    def plane(action, level, wait):
        for first, onward, parity in ((flat, "upright", 1), (upright, "flat", 0)):
            slot = level * width + first
            if wait:
                arrive(slot)

            @pl.when(level % 2 == parity)
            def _():
                action(copy(onward, slot))

            action(copy("twin", slot))

    def far(action, level, wait):
        slot = level * width + corner
        if wait:
            arrive(slot)
        action(copy("twin", slot))

    def around(distance, do):
        if distance == 0:
            do(z, True)
            return

        @pl.when(z >= distance)
        def _():
            do(z - distance, True)

        @pl.when(z + distance < depth)
        def _():
            do(z + distance, False)

    def start(descriptor):
        descriptor.start()

    def finish(descriptor):
        descriptor.wait_send()

    own = pltpu.make_async_copy(piece, gathered.at[z * width + me], local_sem)
    own.start()
    column(start, z, 0, True)

    for turn in range(1, depth + 2):
        if turn < depth:
            def onward(level, rising, turn=turn):
                arrive(level * width + me)
                column(start, level, turn, rising)
            around(turn, onward)
        if turn - 1 < depth:
            around(turn - 1, lambda level, rising: plane(start, level, True))
        if turn >= 2:
            around(turn - 2, lambda level, rising: far(start, level, True))
    for distance in range(depth):
        def rest(level, rising, distance=distance):
            for other in (twin, flat + twin - me, upright + twin - me, corner + twin - me):
                arrive(level * width + other)
            column(finish, level, distance, rising)
            plane(finish, level, False)
            far(finish, level, False)
        around(distance, rest)
    own.wait()


def gather_all(piece):
    depth, width = lax.axis_size("st"), lax.axis_size("mem")
    if width != 8 or depth < 2:
        return lax.all_gather(piece, ("st", "mem"))
    anywhere = pl.BlockSpec(memory_space=pl.ANY)
    return pl.pallas_call(
        gather_kernel,
        out_shape=jax.ShapeDtypeStruct((depth * width, *piece.shape), piece.dtype),
        in_specs=[anywhere],
        out_specs=anywhere,
        scratch_shapes=[
            pltpu.SemaphoreType.DMA((5 * depth * width,)),
            pltpu.SemaphoreType.DMA((depth * width,)),
            pltpu.SemaphoreType.DMA,
        ],
        compiler_params=pltpu.CompilerParams(collective_id=0, has_side_effects=True),
    )(piece)


def gathered_shards(ensemble, obs_values, obs_sigma, obs_operator, block_cols, batch_order):
    size = obs_operator.shape[-1]
    row_count, width = ensemble.shape
    blocks = row_count // size
    mem_count, st_count = lax.axis_size("mem"), lax.axis_size("st")
    members = width * mem_count
    batches, obs_blocks, _ = block_cols.shape
    local = ensemble.reshape(blocks, size, width).transpose(0, 2, 1)
    gathered = gather_all(local)
    place = jnp.stack([lax.axis_index("mem"), lax.axis_index("st")]).astype(jnp.int32)
    smem = pl.BlockSpec(memory_space=pltpu.SMEM)
    vmem = pl.BlockSpec(memory_space=pltpu.VMEM)
    analysis, logw, ess = pl.pallas_call(
        functools.partial(kernel, members),
        out_shape=(
            jax.ShapeDtypeStruct((blocks, width, size), jnp.float32),
            jax.ShapeDtypeStruct((width, 1), jnp.float32),
            jax.ShapeDtypeStruct((1, 1), jnp.float32),
        ),
        in_specs=[smem, smem, smem, vmem, vmem, vmem, pl.BlockSpec(memory_space=pl.ANY)],
        out_specs=(vmem, vmem, vmem),
        scratch_shapes=[
            pltpu.VMEM((st_count * blocks, members, size), jnp.float32),
            pltpu.VMEM((obs_blocks, members, size), jnp.float32),
            pltpu.VMEM((obs_blocks, size), jnp.float32),
            pltpu.VMEM((obs_blocks, size, 2 * size), jnp.float32),
            pltpu.VMEM((size * obs_blocks, size), jnp.float32),
            pltpu.VMEM((PANEL * obs_blocks, size), jnp.float32),
            pltpu.VMEM((members, size), jnp.float32),
            pltpu.VMEM((members, 1), jnp.float32),
            pltpu.SemaphoreType.DMA((mem_count * st_count,)),
        ],
        compiler_params=pltpu.CompilerParams(vmem_limit_bytes=48 << 20),
    )(batch_order, block_cols, place, obs_values, obs_sigma, obs_operator, gathered)
    states = analysis.transpose(0, 2, 1).reshape(row_count, width)
    return states, logw.reshape(width), ess.reshape(())


def solve_blocks(moment, target):
    factor = jnp.linalg.cholesky(moment)
    return jax.vmap(lambda lower, right: jax.scipy.linalg.cho_solve((lower, True), right))(
        factor, target
    )


def reduced_shards(ensemble, obs_values, obs_sigma, obs_operator, block_cols, batch_order):
    block_size = obs_operator.shape[-1]
    row_count, mem_dev = ensemble.shape
    nblocks = row_count // block_size
    members = mem_dev * lax.axis_size("mem")
    batches, obs_blocks, col_count = block_cols.shape
    temper = 1.0 / math.sqrt(batches * obs_blocks * block_size)
    offset = lax.axis_index("st") * nblocks
    states = ensemble.reshape(nblocks, block_size, mem_dev)
    eye = jnp.eye(block_size, dtype=jnp.float32)
    slots = jnp.arange(nblocks, dtype=jnp.int32)
    loglik = jnp.zeros((mem_dev,), jnp.float32)
    for batch_step in range(batches):
        chosen = batch_order[batch_step]
        operator_now = lax.dynamic_index_in_dim(obs_operator, chosen, 0, keepdims=False)
        columns = lax.dynamic_index_in_dim(block_cols, chosen, 0, keepdims=False)
        values_now = lax.dynamic_index_in_dim(obs_values, chosen, 0, keepdims=False)
        sigma_now = lax.dynamic_index_in_dim(obs_sigma, chosen, 0, keepdims=False)
        local_ids = columns.reshape(-1) - offset
        selector = (local_ids[:, None] == slots[None, :]).astype(jnp.float32)
        picked = jnp.einsum("ps,sim->pim", selector, states, precision=precise)
        picked = picked.reshape(obs_blocks, col_count, block_size, mem_dev)
        partial_value = jnp.einsum("bkij,bkjm->bim", operator_now, picked, precision=precise)
        image = lax.psum(partial_value, "st")
        misfit = (values_now[:, :, None] - image) / sigma_now[:, :, None]
        loglik = loglik - 0.5 * temper * jnp.sum(misfit * misfit, axis=(0, 1))
        center = lax.psum(jnp.sum(image, axis=2), "mem") / members
        anomaly = image - center[:, :, None]
        moment_sum, cross_sum = lax.psum(
            (
                jnp.einsum("bim,bjm->bij", anomaly, anomaly, precision=precise),
                jnp.einsum("bkim,bjm->bkij", picked, anomaly, precision=precise),
            ),
            "mem",
        )
        moment = moment_sum / (members - 1) + eye * (sigma_now * sigma_now)[:, :, None]
        cross = cross_sum / (members - 1)
        target = (values_now - center)[:, :, None] - 0.5 * anomaly
        weights = solve_blocks(moment, target)
        change = jnp.einsum("bkij,bjm->bkim", cross, weights, precision=precise)
        change = change.reshape(obs_blocks * col_count, block_size, mem_dev)
        states = states + jnp.einsum("ps,pim->sim", selector, change, precision=precise)
    largest_local = jnp.max(loglik)
    largest = lax.pmax(largest_local, "mem")
    scaled = jnp.exp(loglik - largest)
    summed, squares = lax.psum((jnp.sum(scaled), jnp.sum(scaled * scaled)), "mem")
    log_weights = loglik - largest - jnp.log(summed)
    ess = summed * summed / squares
    return (states.reshape(row_count, mem_dev), log_weights, ess)


def shards(ensemble, *others):
    devices = lax.axis_size("mem") * lax.axis_size("st")
    fits = 4 * ensemble.size * devices <= GATHER_LIMIT
    return (gathered_shards if fits else reduced_shards)(ensemble, *others)


def solution(mesh):
    placed = (P("st", "mem"), P(), P(), P(), P(), P())
    return jax.shard_map(
        shards,
        mesh=mesh,
        in_specs=placed,
        out_specs=(P("st", "mem"), P("mem"), P()),
        check_vma=False,
    )
```
